32 devices in a mesh: obs: 4 (over z), src: 8 (over y, x, core).
Axes of the slice: x: 2, y: 2, z: 4, core: 2. Of those that a mesh axis runs over, the one named last changes fastest.
Arguments:
- history: bfloat16 [3, 64, 64, 1536], P(None, ('obs', 'src')), may hold values from -6 to 6
- incident: bfloat16 [5, 64, 64, 1536], P(None, ('obs', 'src')), may hold values from -6 to 6
- proj_basis: bfloat16 [64, 64, 1536], P(('obs', 'src')), may hold values from -0.15625 to 0.15625
- expand_basis: bfloat16 [64, 64, 1536], P(('obs', 'src')), may hold values from -0.75 to 0.75
- near_inverse: bfloat16 [64, 1536, 1536], P(('obs', 'src')), may hold values from -0.15625 to 0.15625
- couplings: bfloat16 [2, 4096, 4, 8, 128], P(None, 'obs', None, 'src'), may hold values from -0.09375 to 0.09375
- lags: int32 [64, 4, 8, 2], P('obs', None, 'src'), may hold values from 0 to 2, as said below
Outputs:
- currents: bfloat16 [5, 64, 64, 1536], P(None, ('obs', 'src'))
The draws below stay inside these ranges and needn't reach their ends.
Inputs may be any that keep to these rules, and one draw needn't show every extreme that they name: lags[j, o, s, k] is the lag from source cluster j to observer cluster (o * 8 + s) * 2 + k. Entries are 0, 1 or 2, and the entry of every cluster with itself is 0.
All inputs are finite; a program needn't handle non-finite values.
Results may differ from the reference program's by a relative error of at most 0.025.
Values may be sent and summed in bfloat16 or wider, within the bound.
A program may use at most 192 MiB of HBM per device.

```python
import math
import jax
import jax.numpy as jnp
from jax import lax

CL_DEV = 2
B = 1536
R = 64
E = 64
STEPS = 5
TAPS = 2
HIST = 3
C = 64
N_OBS = 4
N_SRC = 8


def draw_lags(key, part):
    shape = (C, N_OBS, N_SRC, CL_DEV)
    raw_value = jax.random.randint(key, shape, 0, 8)
    lag_value = jnp.where(raw_value == 0, 0, jnp.where(raw_value <= 4, 1, 2))
    source = lax.broadcasted_iota(jnp.int32, shape, 0)
    observer = (lax.broadcasted_iota(jnp.int32, shape, 1) * N_SRC + lax.broadcasted_iota(jnp.int32, shape, 2)) * CL_DEV + lax.broadcasted_iota(jnp.int32, shape, 3)
    return jnp.where(source == observer, 0, lag_value).astype(jnp.int32)


def strengthened(array, stream_key, source, target, parts, factor):
    owner, partner = [(jnp.arange(array.shape[axis_at]) // (array.shape[axis_at] // parts)).reshape([-1 if axis == axis_at else 1 for axis in range(array.ndim)]) for axis_at in (source, target)]
    chosen = jax.random.permutation(stream_key, parts)[partner]
    strong = (owner == chosen) | (owner == (partner + parts // 2) % parts)
    return jnp.where(strong, factor * array, array)


def block_levels(rng, dims, shards, low, top_value):
    def one(position, blocks):
        draws = jax.random.uniform(jax.random.fold_in(jax.random.fold_in(rng, 6), position), (blocks,), jnp.float32, low / len(shards), top_value / len(shards))
        return jnp.repeat(jnp.exp(draws), dims[position] // blocks).reshape((-1,) + (1,) * (len(dims) - position - 1))

    factor_of = one(*shards[0])
    for cut in shards[1:]:
        factor_of = factor_of * one(*cut)
    return factor_of


def bell_draw(own_key, shape, spread, most, shards=(), kind=jnp.bfloat16):
    drawn = jax.random.normal(own_key, shape, jnp.float32) * spread
    if len(shards) > 0:
        drawn = block_levels(own_key, shape, shards, -0.22, 0.18) * drawn
    return jnp.clip(drawn, min=-most, max=most).astype(kind)


def heavy_noise(key, shape, scale, limit, shards, heavy, held_as=jnp.bfloat16):
    drawn = scale * jax.random.normal(key, shape, jnp.float32)
    if shards:
        drawn = drawn * block_levels(key, shape, shards, -0.22, 0.18)
    return jnp.clip(strengthened(drawn, jax.random.fold_in(key, 3), *heavy), -limit, limit).astype(held_as)


def setup_inputs(seed: int = 0) -> dict:
    seeds = jax.random.split(jax.random.key(seed), 8)
    history = bell_draw(seeds[0], (HIST, C, E, B), 1.0, 6.0, ((1, 32),))
    incident = bell_draw(seeds[1], (STEPS, C, E, B), 1.0, 6.0, ((1, 32),))
    proj_basis = bell_draw(seeds[2], (C, R, B), B ** -0.5, 0.15625, ((0, 32),))
    expand_basis = bell_draw(seeds[3], (C, R, B), R ** -0.5, 0.75, ((0, 32),))
    near_inverse = bell_draw(seeds[4], (C, B, B), B ** -0.5, 0.15625, ((0, 32),))
    couplings = heavy_noise(seeds[5], (TAPS, C * R, N_OBS, N_SRC, CL_DEV * R), (2 * C * R) ** -0.5, 0.09375, ((1, 4), (3, 8)), (1, 2, 4, 2.0))
    lags = draw_lags(jax.random.fold_in(seeds[7], 71), 0)
    return dict(history=history, incident=incident, proj_basis=proj_basis, expand_basis=expand_basis, near_inverse=near_inverse, couplings=couplings, lags=lags)


def project(current, proj_basis):
    projected = jnp.einsum('ceb,crb->ecr', current.astype(jnp.float32), proj_basis.astype(jnp.float32), precision=lax.Precision.HIGHEST)
    return projected.astype(jnp.bfloat16).reshape(E, C * R)


def far_sum(stacked, kernel, lag_pairs):
    group_size = math.gcd(C, 16)
    block_count = C // group_size

    def one_block(block_index):
        start = (block_index * group_size).astype(jnp.int32)
        block_kernel = lax.dynamic_slice_in_dim(kernel, (start * R).astype(jnp.int32), group_size * R, 2)
        block_kernel = block_kernel.reshape(TAPS, C, R, group_size, R)
        block_lags = lax.dynamic_slice_in_dim(lag_pairs, start, group_size, 1)
        total = jnp.zeros((E, group_size * R), jnp.float32)
        for delay in range(1, HIST + 1):
            combined = jnp.zeros((C, R, group_size, R), jnp.bfloat16)
            for tap_index in range(TAPS):
                if delay - tap_index >= 1:
                    chosen = (block_lags == delay - tap_index)[:, None, :, None]
                    combined = jnp.where(chosen, block_kernel[tap_index], combined)
            total = total + jnp.dot(stacked[delay - 1], combined.reshape(C * R, group_size * R).astype(jnp.float32), precision=lax.Precision.HIGHEST)
        return total

    blocks = lax.map(one_block, jnp.arange(block_count, dtype=jnp.int32))
    return jnp.transpose(blocks, (1, 0, 2)).reshape(E, C * R)


def reference(history, incident, proj_basis, expand_basis, near_inverse, couplings, lags):
    kernel = couplings.reshape(TAPS, C * R, C * R)
    lag_pairs = lags.reshape(C, C)
    past = [project(history[slot_index], proj_basis) for slot_index in range(HIST)]
    results = []
    for step in range(STEPS):
        stacked = jnp.stack([past[len(past) - delay] for delay in range(1, HIST + 1)]).astype(jnp.float32)
        field = far_sum(stacked, kernel, lag_pairs).astype(jnp.bfloat16).reshape(E, C, R)
        far_field = jnp.einsum('ecr,crb->ceb', field.astype(jnp.float32), expand_basis.astype(jnp.float32), precision=lax.Precision.HIGHEST)
        residual_field = (incident[step].astype(jnp.float32) - far_field).astype(jnp.bfloat16)

        def near_apply(pair):
            return jnp.dot(pair[0].astype(jnp.float32), pair[1].astype(jnp.float32), precision=lax.Precision.HIGHEST)

        current = lax.map(near_apply, (residual_field, near_inverse)).astype(jnp.bfloat16)
        results.append(current)
        past.append(project(current, proj_basis))
    return jnp.stack(results)
```

```python
import functools

import jax
import jax.numpy as jnp
from jax import lax
from jax.experimental import pallas as pl
from jax.experimental.pallas import tpu as pltpu
from jax.sharding import PartitionSpec as P

MESH = pl.DeviceIdType.MESH
F32 = jnp.float32
BF16 = jnp.bfloat16
NT = (((1,), (1,)), ((), ()))


def flipped(me, bits, count):
    other = me
    place = 1
    while place < count:
        if bits & place:
            other = other + (1 - 2 * ((me // place) % 2)) * place
        place *= 2
    return other


def partner(me, turn, count):
    if count & (count - 1) == 0:
        return flipped(me, count - turn, count)
    return lax.rem(me + turn, count)


def kernel(n_obs, n_src, hist_ref, inc_ref, proj_ref, expand_ref, near_ref, coup_ref, lag_ref, out_ref,
           hv, av, pv, nv, cv, cf, wv, yv, xn, bv, mv, qh, qn, sendp, recvp, base, ov,
           load_sem, out_sem, hs_sem, hr_sem, qs_sem, qr_sem, ps_sem, pr_sem):
    o = lax.axis_index("obs")
    s = lax.axis_index("src")
    hist, clusters, excite, unknowns = hist_ref.shape
    steps = inc_ref.shape[0]
    rank = proj_ref.shape[1]
    width = clusters * rank
    sources = lag_ref.shape[2]
    tile = 256

    loads = []

    def load(src, dst):
        copy = pltpu.make_async_copy(src, dst, load_sem.at[len(loads)])
        copy.start()
        loads.append(copy)
        return copy

    def rows(index, size):
        return pl.ds(index * size, size)

    h_loads = [load(proj_ref.at[c], pv.at[c, rows(c, rank)]) for c in range(clusters)]
    h_loads += [load(hist_ref.at[k, c], hv.at[c, rows(k, excite)]) for c in range(clusters) for k in range(hist)]
    c_loads = [load(coup_ref, cv)]
    n_loads = []
    for c in range(clusters):
        mine = [load(inc_ref.at[t, c], av.at[c, rows(t, excite)]) for t in range(steps)]
        mine.append(load(expand_ref.at[c], av.at[c, rows(steps, excite)]))
        mine.append(load(near_ref.at[c], nv.at[c]))
        n_loads.append(mine)

    barrier = pltpu.get_barrier_semaphore()
    src_peers = [partner(s, turn, n_src) for turn in range(1, n_src)]
    obs_peers = [partner(o, turn, n_obs) for turn in range(1, n_obs)]
    for peer in src_peers:
        pl.semaphore_signal(barrier, inc=1, device_id=(o, peer), device_id_type=MESH)
    for peer in obs_peers:
        pl.semaphore_signal(barrier, inc=1, device_id=(peer, s), device_id_type=MESH)

    for c in range(clusters):
        for k in range(clusters):
            if k != c:
                pv[c, k * rank:(k + 1) * rank] = jnp.zeros((rank, unknowns), BF16)
                xn[c, k * rank:(k + 1) * rank] = jnp.zeros((rank, unknowns), BF16)

    for copy in h_loads:
        copy.wait()
    past = jnp.zeros((hist * excite, width), F32)
    for c in range(clusters):
        past = past + lax.dot_general(hv[c], pv[c], NT, preferred_element_type=F32)
    qh[s] = past.astype(BF16)
    pl.semaphore_wait(barrier, n_src + n_obs - 2)

    def h_copy(turn, slot):
        return pltpu.make_async_remote_copy(
            src_ref=qh.at[slot], dst_ref=qh.at[slot], send_sem=hs_sem.at[turn], recv_sem=hr_sem.at[slot],
            device_id=(o, src_peers[turn]), device_id_type=MESH)

    def q_copy(step, turn, slot):
        return pltpu.make_async_remote_copy(
            src_ref=qn.at[step, slot], dst_ref=qn.at[step, slot], send_sem=qs_sem.at[step, turn],
            recv_sem=qr_sem.at[step, slot], device_id=(o, src_peers[turn]), device_id_type=MESH)

    def p_copy(step, turn, at, slot):
        return pltpu.make_async_remote_copy(
            src_ref=sendp.at[step, at], dst_ref=recvp.at[step, slot], send_sem=ps_sem.at[step, turn],
            recv_sem=pr_sem.at[step, slot], device_id=(obs_peers[turn], s), device_id_type=MESH)

    for turn in range(n_src - 1):
        h_copy(turn, s).start()

    for copy in c_loads:
        copy.wait()
    lane = lax.broadcasted_iota(jnp.int32, (rank, width), 1)

    def build(j, carry):
        for p in range(2):
            cf[p] = cv[p, pl.ds(pl.multiple_of(j * (rank * n_obs), rank * n_obs), rank * n_obs), :].astype(F32)
        at = pl.ds(pl.multiple_of(j * rank, rank), rank)
        for to in range(n_obs):
            lag = jnp.full((rank, width), lag_ref[to, 0, j], jnp.int32)
            for k in range(1, clusters):
                lag = jnp.where(lane >= k * rank, lag_ref[to, k, j], lag)
            first = cf[0, pl.ds(to, rank, stride=n_obs), :]
            second = cf[1, pl.ds(to, rank, stride=n_obs), :]
            zero = jnp.zeros_like(first)
            one, two = lag == 1, lag == 2
            cols = slice(to * width, (to + 1) * width)
            wv[0, at, cols] = jnp.where(one, first, zero).astype(BF16)
            wv[1, at, cols] = jnp.where(two, first, jnp.where(one, second, zero)).astype(BF16)
            wv[2, at, cols] = jnp.where(two, second, zero).astype(BF16)
        return carry

    lax.fori_loop(0, sources, build, 0)

    def near(c):
        for copy in n_loads[c]:
            copy.wait()

        def column(j, carry):
            at = pl.ds(pl.multiple_of(j * tile, tile), tile)
            value = jnp.dot(av[c], nv[c, :, at], preferred_element_type=F32)
            yv[c, :, at] = value
            xn[c, c * rank:(c + 1) * rank, at] = value[steps * excite:].astype(BF16)
            return carry

        lax.fori_loop(0, unknowns // tile, column, 0)
        return lax.dot_general(yv[c].astype(BF16), pv[c], NT, preferred_element_type=F32)

    def keep(c, value):
        if c == 0:
            bv[...] = value[:steps * excite]
        else:
            bv[...] += value[:steps * excite]
        mv[c * rank:(c + 1) * rank] = value[steps * excite:].astype(BF16)

    keep(0, near(0))

    for turn in range(n_src - 1):
        h_copy(turn, src_peers[turn]).wait_recv()

    def gathered(ref):
        return jnp.concatenate([ref[k] for k in range(n_src)], axis=1)

    def slot_of(ref, k):
        return jnp.concatenate([ref[j, k * excite:(k + 1) * excite] for j in range(n_src)], axis=1)

    older = [slot_of(qh, k) for k in range(hist)]

    def send_partial(step, total):
        for to in range(n_obs):
            sendp[step, to] = total[:, to * width:(to + 1) * width].astype(BF16)
        for turn in range(n_obs - 1):
            p_copy(step, turn, obs_peers[turn], o).start()

    total = jnp.dot(older[hist - 1], wv[0], preferred_element_type=F32)
    for d in range(2, hist + 1):
        total = total + jnp.dot(older[hist - d], wv[d - 1], preferred_element_type=F32)
    send_partial(0, total)

    for ahead in range(1, hist):
        total = None
        for d in range(ahead + 1, hist + 1):
            term = jnp.dot(older[hist + ahead - d], wv[d - 1], preferred_element_type=F32)
            total = term if total is None else total + term
        base[ahead] = total
    for ahead in range(hist, steps):
        base[ahead] = jnp.zeros((excite, n_obs * width), F32)

    for c in range(1, clusters):
        keep(c, near(c))

    outs = []

    def finish(step, field):
        for c in range(clusters):
            far = jnp.dot(field, xn[c], preferred_element_type=F32)
            ov[step, c] = (yv[c, step * excite:(step + 1) * excite] - far).astype(BF16)
            copy = pltpu.make_async_copy(ov.at[step, c], out_ref.at[step, c], out_sem.at[step, c])
            copy.start()
            outs.append(copy)

    for step in range(steps):
        field = sendp[step, o].astype(F32)
        for turn in range(n_obs - 1):
            p_copy(step, turn, 0, obs_peers[turn]).wait_recv()
            field = field + recvp[step, obs_peers[turn]].astype(F32)
        field = field.astype(BF16)
        if step + 1 == steps:
            finish(step, field)
            break
        newest = bv[step * excite:(step + 1) * excite] - jnp.dot(field, mv[...], preferred_element_type=F32)
        qn[step, s] = newest.astype(BF16)
        for turn in range(n_src - 1):
            q_copy(step, turn, s).start()
        finish(step, field)
        for turn in range(n_src - 1):
            q_copy(step, turn, src_peers[turn]).wait_recv()
        columns = gathered(qn.at[step])
        send_partial(step + 1, base[step + 1] + jnp.dot(columns, wv[0], preferred_element_type=F32))
        for d in range(2, hist + 1):
            if step + d < steps:
                base[step + d] += jnp.dot(columns, wv[d - 1], preferred_element_type=F32)

    for copy in outs:
        copy.wait()
    for turn in range(n_src - 1):
        h_copy(turn, s).wait_send()
    for step in range(steps):
        for turn in range(n_obs - 1):
            p_copy(step, turn, obs_peers[turn], o).wait_send()
        if step + 1 < steps:
            for turn in range(n_src - 1):
                q_copy(step, turn, s).wait_send()


def per_device(n_obs, n_src, history, incident, proj_basis, expand_basis, near_inverse, couplings, lags):
    hist, clusters, excite, unknowns = history.shape
    steps = incident.shape[0]
    rank = proj_basis.shape[1]
    width = clusters * rank
    taps, src_rows = couplings.shape[:2]
    sources = lags.shape[0]
    obs_cols = n_obs * width
    flat = couplings.reshape(taps, src_rows * n_obs, width)
    lag_table = jnp.transpose(lags.reshape(sources, n_obs, clusters), (1, 2, 0))
    stacked = (steps + 1) * excite
    loads = clusters * (1 + hist + steps + 2) + 1
    any_spec = pl.BlockSpec(memory_space=pl.ANY)
    dma = pltpu.SemaphoreType.DMA
    return pl.pallas_call(
        functools.partial(kernel, n_obs, n_src),
        out_shape=jax.ShapeDtypeStruct(incident.shape, BF16),
        in_specs=[any_spec] * 6 + [pl.BlockSpec(memory_space=pltpu.SMEM)],
        out_specs=any_spec,
        scratch_shapes=[
            pltpu.VMEM((clusters, hist * excite, unknowns), BF16),
            pltpu.VMEM((clusters, stacked, unknowns), BF16),
            pltpu.VMEM((clusters, width, unknowns), BF16),
            pltpu.VMEM((clusters, unknowns, unknowns), BF16),
            pltpu.VMEM((taps, src_rows * n_obs, width), BF16),
            pltpu.VMEM((taps, rank * n_obs, width), F32),
            pltpu.VMEM((hist, src_rows, obs_cols), BF16),
            pltpu.VMEM((clusters, stacked, unknowns), F32),
            pltpu.VMEM((clusters, width, unknowns), BF16),
            pltpu.VMEM((steps * excite, width), F32),
            pltpu.VMEM((width, width), BF16),
            pltpu.VMEM((n_src, hist * excite, width), BF16),
            pltpu.VMEM((steps - 1, n_src, excite, width), BF16),
            pltpu.VMEM((steps, n_obs, excite, width), BF16),
            pltpu.VMEM((steps, n_obs, excite, width), BF16),
            pltpu.VMEM((steps, excite, obs_cols), F32),
            pltpu.VMEM((steps, clusters, excite, unknowns), BF16),
            dma((loads,)),
            dma((steps, clusters)),
            dma((n_src,)),
            dma((n_src,)),
            dma((steps - 1, n_src)),
            dma((steps - 1, n_src)),
            dma((steps, n_obs)),
            dma((steps, n_obs)),
        ],
        compiler_params=pltpu.CompilerParams(
            collective_id=0, has_side_effects=True, vmem_limit_bytes=63000 * 1024
        ),
    )(history, incident, proj_basis, expand_basis, near_inverse, flat, lag_table)


def solution(mesh):
    placed = (
        P(None, ("obs", "src"), None, None),
        P(None, ("obs", "src"), None, None),
        P(("obs", "src"), None, None),
        P(("obs", "src"), None, None),
        P(("obs", "src"), None, None),
        P(None, "obs", None, "src", None),
        P("obs", None, "src", None),
    )
    return jax.shard_map(
        functools.partial(per_device, mesh.shape["obs"], mesh.shape["src"]),
        mesh=mesh,
        in_specs=placed,
        out_specs=P(None, ("obs", "src"), None, None),
        check_vma=False,
    )
```

```python
import functools

import jax
import jax.numpy as jnp
from jax import lax
from jax.experimental import pallas as pl
from jax.experimental.pallas import tpu as pltpu
from jax.sharding import PartitionSpec as P

MESH = pl.DeviceIdType.MESH
F32 = jnp.float32
BF16 = jnp.bfloat16
NT = (((1,), (1,)), ((), ()))


def flipped(me, bits, count):
    other = me
    place = 1
    while place < count:
        if bits & place:
            other = other + (1 - 2 * ((me // place) % 2)) * place
        place *= 2
    return other


def partner(me, turn, count):
    if count & (count - 1) == 0:
        return flipped(me, count - turn, count)
    return lax.rem(me + turn, count)


def kernel(n_obs, n_src, hist_ref, inc_ref, proj_ref, expand_ref, near_ref, coup_ref, lag_ref, out_ref,
           hv, av, pv, nv, cv, cf, wv, yv, xn, bv, mv, qh, qn, sendp, recvp, base, ov,
           load_sem, out_sem, hs_sem, hr_sem, qs_sem, qr_sem, ps_sem, pr_sem):
    o = lax.axis_index("obs")
    s = lax.axis_index("src")
    hist, clusters, excite, unknowns = hist_ref.shape
    steps = inc_ref.shape[0]
    rank = proj_ref.shape[1]
    width = clusters * rank
    sources = lag_ref.shape[2]
    tile = 256

    barrier = pltpu.get_barrier_semaphore()
    src_peers = [partner(s, turn, n_src) for turn in range(1, n_src)]
    obs_peers = [partner(o, turn, n_obs) for turn in range(1, n_obs)]
    for peer in src_peers:
        pl.semaphore_signal(barrier, inc=1, device_id=(o, peer), device_id_type=MESH)
    for peer in obs_peers:
        pl.semaphore_signal(barrier, inc=1, device_id=(peer, s), device_id_type=MESH)

    loads = []

    def load(src, dst):
        copy = pltpu.make_async_copy(src, dst, load_sem.at[len(loads)])
        copy.start()
        loads.append(copy)
        return copy

    def rows(index, size):
        return pl.ds(index * size, size)

    h_loads = [load(proj_ref.at[c], pv.at[c, rows(c, rank)]) for c in range(clusters)]
    h_loads += [load(hist_ref.at[k, c], hv.at[c, rows(k, excite)]) for c in range(clusters) for k in range(hist)]
    c_loads = [load(coup_ref, cv)]
    n_loads = []
    for c in range(clusters):
        mine = [load(inc_ref.at[t, c], av.at[c, rows(t, excite)]) for t in range(steps)]
        mine.append(load(expand_ref.at[c], av.at[c, rows(steps, excite)]))
        mine.append(load(near_ref.at[c], nv.at[c]))
        n_loads.append(mine)

    for c in range(clusters):
        for k in range(clusters):
            if k != c:
                pv[c, k * rank:(k + 1) * rank] = jnp.zeros((rank, unknowns), BF16)
                xn[c, k * rank:(k + 1) * rank] = jnp.zeros((rank, unknowns), BF16)

    for copy in h_loads:
        copy.wait()
    past = jnp.zeros((hist * excite, width), F32)
    for c in range(clusters):
        past = past + lax.dot_general(hv[c], pv[c], NT, preferred_element_type=F32)
    qh[s] = past.astype(BF16)
    pl.semaphore_wait(barrier, n_src + n_obs - 2)

    def h_copy(turn, slot):
        return pltpu.make_async_remote_copy(
            src_ref=qh.at[slot], dst_ref=qh.at[slot], send_sem=hs_sem.at[turn], recv_sem=hr_sem.at[slot],
            device_id=(o, src_peers[turn]), device_id_type=MESH)

    def q_copy(step, turn, slot):
        return pltpu.make_async_remote_copy(
            src_ref=qn.at[step, slot], dst_ref=qn.at[step, slot], send_sem=qs_sem.at[step, turn],
            recv_sem=qr_sem.at[step, slot], device_id=(o, src_peers[turn]), device_id_type=MESH)

    def p_copy(step, turn, at, slot):
        return pltpu.make_async_remote_copy(
            src_ref=sendp.at[step, at], dst_ref=recvp.at[step, slot], send_sem=ps_sem.at[step, turn],
            recv_sem=pr_sem.at[step, slot], device_id=(obs_peers[turn], s), device_id_type=MESH)

    group = 2 if n_src % 2 == 0 else 1
    relayed = group == 2 and n_src & (n_src - 1) == 0
    beside = n_src - 2
    direct = [turn for turn in range(n_src - 1) if not relayed or turn == beside or (n_src - 1 - turn) % 2 == 0]
    far = [turn for turn in direct if turn != beside] if relayed else []
    for turn in direct:
        h_copy(turn, s).start()

    for copy in c_loads:
        copy.wait()
    lane = lax.broadcasted_iota(jnp.int32, (rank, width), 1)

    def build(j, carry):
        for p in range(2):
            cf[p] = cv[p, pl.ds(pl.multiple_of(j * (rank * n_obs), rank * n_obs), rank * n_obs), :].astype(F32)
        at = pl.ds(pl.multiple_of(j * rank, rank), rank)
        for to in range(n_obs):
            lag = jnp.full((rank, width), lag_ref[to, 0, j], jnp.int32)
            for k in range(1, clusters):
                lag = jnp.where(lane >= k * rank, lag_ref[to, k, j], lag)
            first = cf[0, pl.ds(to, rank, stride=n_obs), :]
            second = cf[1, pl.ds(to, rank, stride=n_obs), :]
            zero = jnp.zeros_like(first)
            one, two = lag == 1, lag == 2
            cols = slice(to * width, (to + 1) * width)
            wv[0, at, cols] = jnp.where(one, first, zero).astype(BF16)
            wv[1, at, cols] = jnp.where(two, first, jnp.where(one, second, zero)).astype(BF16)
            wv[2, at, cols] = jnp.where(two, second, zero).astype(BF16)
        return carry

    lax.fori_loop(0, sources, build, 0)

    def near(c):
        for copy in n_loads[c]:
            copy.wait()

        def column(j, carry):
            at = pl.ds(pl.multiple_of(j * tile, tile), tile)
            value = jnp.dot(av[c], nv[c, :, at], preferred_element_type=F32)
            yv[c, :, at] = value
            xn[c, c * rank:(c + 1) * rank, at] = value[steps * excite:].astype(BF16)
            return carry

        lax.fori_loop(0, unknowns // tile, column, 0)
        return lax.dot_general(yv[c].astype(BF16), pv[c], NT, preferred_element_type=F32)

    def keep(c, value):
        if c == 0:
            bv[...] = value[:steps * excite]
        else:
            bv[...] += value[:steps * excite]
        mv[c * rank:(c + 1) * rank] = value[steps * excite:].astype(BF16)

    def forward(turn):
        return pltpu.make_async_remote_copy(
            src_ref=qh.at[src_peers[turn]], dst_ref=qh.at[src_peers[turn]], send_sem=hs_sem.at[turn - 1],
            recv_sem=hr_sem.at[src_peers[turn]], device_id=(o, src_peers[beside]), device_id_type=MESH)

    for turn in reversed(far):
        h_copy(turn, src_peers[turn]).wait_recv()
        forward(turn).start()
    for turn in range(n_src - 1):
        if turn not in far:
            h_copy(turn, src_peers[turn]).wait_recv()

    pairs = n_src // group
    own_pair = s // group
    ordered = [own_pair] + [partner(own_pair, turn, pairs) for turn in range(pairs - 1, 0, -1)]

    def gathered(ref):
        return jnp.concatenate([ref[k] for k in range(n_src)], axis=1)

    def newest_term(step, total):
        for place, pair in enumerate(ordered):
            for k in range(group):
                if place > 0:
                    q_copy(step, 0, pair * group + k).wait_recv()
                elif group == 2 and k == 0:
                    q_copy(step, 0, partner_slot).wait_recv()
            part = jnp.concatenate([qn[step, pair * group + k] for k in range(group)], axis=1)
            deep = group * width
            rows_at = pl.ds(pl.multiple_of(pair * deep, deep), deep)
            total = total + jnp.dot(part, wv[0, rows_at, :], preferred_element_type=F32)
        return total

    partner_slot = own_pair * 2 + (1 - s % 2)

    def slot_of(ref, k):
        return jnp.concatenate([ref[j, k * excite:(k + 1) * excite] for j in range(n_src)], axis=1)

    older = [slot_of(qh, k) for k in range(hist)]

    def send_partial(step, total):
        for to in range(n_obs):
            sendp[step, to] = total[:, to * width:(to + 1) * width].astype(BF16)
        for turn in range(n_obs - 1):
            p_copy(step, turn, obs_peers[turn], o).start()

    total = jnp.dot(older[hist - 1], wv[0], preferred_element_type=F32)
    for d in range(2, hist + 1):
        total = total + jnp.dot(older[hist - d], wv[d - 1], preferred_element_type=F32)
    send_partial(0, total)

    for ahead in range(1, hist):
        total = None
        for d in range(ahead + 1, hist + 1):
            term = jnp.dot(older[hist + ahead - d], wv[d - 1], preferred_element_type=F32)
            total = term if total is None else total + term
        base[ahead] = total
    for ahead in range(hist, steps):
        base[ahead] = jnp.zeros((excite, n_obs * width), F32)

    for c in range(clusters):
        keep(c, near(c))

    outs = []

    def finish(step, field):
        for c in range(clusters):
            far = jnp.dot(field, xn[c], preferred_element_type=F32)
            ov[step, c] = (yv[c, step * excite:(step + 1) * excite] - far).astype(BF16)
            copy = pltpu.make_async_copy(ov.at[step, c], out_ref.at[step, c], out_sem.at[step, c])
            copy.start()
            outs.append(copy)

    for step in range(steps):
        field = sendp[step, o].astype(F32)
        for turn in range(n_obs - 1):
            p_copy(step, turn, 0, obs_peers[turn]).wait_recv()
            field = field + recvp[step, obs_peers[turn]].astype(F32)
        field = field.astype(BF16)
        if step + 1 == steps:
            finish(step, field)
            break
        newest = bv[step * excite:(step + 1) * excite] - jnp.dot(field, mv[...], preferred_element_type=F32)
        qn[step, s] = newest.astype(BF16)
        for turn in range(n_src - 1):
            q_copy(step, turn, s).start()
        finish(step, field)
        send_partial(step + 1, newest_term(step, base[step + 1]))
        columns = gathered(qn.at[step])
        for d in range(2, hist + 1):
            if step + d < steps:
                base[step + d] += jnp.dot(columns, wv[d - 1], preferred_element_type=F32)

    for copy in outs:
        copy.wait()
    for turn in direct:
        h_copy(turn, s).wait_send()
    for turn in far:
        forward(turn).wait_send()
    for step in range(steps):
        for turn in range(n_obs - 1):
            p_copy(step, turn, obs_peers[turn], o).wait_send()
        if step + 1 < steps:
            for turn in range(n_src - 1):
                q_copy(step, turn, s).wait_send()


def per_device(n_obs, n_src, history, incident, proj_basis, expand_basis, near_inverse, couplings, lags):
    hist, clusters, excite, unknowns = history.shape
    steps = incident.shape[0]
    rank = proj_basis.shape[1]
    width = clusters * rank
    taps, src_rows = couplings.shape[:2]
    sources = lags.shape[0]
    obs_cols = n_obs * width
    flat = couplings.reshape(taps, src_rows * n_obs, width)
    lag_table = jnp.transpose(lags.reshape(sources, n_obs, clusters), (1, 2, 0))
    stacked = (steps + 1) * excite
    loads = clusters * (1 + hist + steps + 2) + 1
    any_spec = pl.BlockSpec(memory_space=pl.ANY)
    dma = pltpu.SemaphoreType.DMA
    return pl.pallas_call(
        functools.partial(kernel, n_obs, n_src),
        out_shape=jax.ShapeDtypeStruct(incident.shape, BF16),
        in_specs=[any_spec] * 6 + [pl.BlockSpec(memory_space=pltpu.SMEM)],
        out_specs=any_spec,
        scratch_shapes=[
            pltpu.VMEM((clusters, hist * excite, unknowns), BF16),
            pltpu.VMEM((clusters, stacked, unknowns), BF16),
            pltpu.VMEM((clusters, width, unknowns), BF16),
            pltpu.VMEM((clusters, unknowns, unknowns), BF16),
            pltpu.VMEM((taps, src_rows * n_obs, width), BF16),
            pltpu.VMEM((taps, rank * n_obs, width), F32),
            pltpu.VMEM((hist, src_rows, obs_cols), BF16),
            pltpu.VMEM((clusters, stacked, unknowns), F32),
            pltpu.VMEM((clusters, width, unknowns), BF16),
            pltpu.VMEM((steps * excite, width), F32),
            pltpu.VMEM((width, width), BF16),
            pltpu.VMEM((n_src, hist * excite, width), BF16),
            pltpu.VMEM((steps - 1, n_src, excite, width), BF16),
            pltpu.VMEM((steps, n_obs, excite, width), BF16),
            pltpu.VMEM((steps, n_obs, excite, width), BF16),
            pltpu.VMEM((steps, excite, obs_cols), F32),
            pltpu.VMEM((steps, clusters, excite, unknowns), BF16),
            dma((loads,)),
            dma((steps, clusters)),
            dma((n_src,)),
            dma((n_src,)),
            dma((steps - 1, n_src)),
            dma((steps - 1, n_src)),
            dma((steps, n_obs)),
            dma((steps, n_obs)),
        ],
        compiler_params=pltpu.CompilerParams(
            collective_id=0, has_side_effects=True, vmem_limit_bytes=63000 * 1024
        ),
    )(history, incident, proj_basis, expand_basis, near_inverse, flat, lag_table)


def solution(mesh):
    placed = (
        P(None, ("obs", "src"), None, None),
        P(None, ("obs", "src"), None, None),
        P(("obs", "src"), None, None),
        P(("obs", "src"), None, None),
        P(("obs", "src"), None, None),
        P(None, "obs", None, "src", None),
        P("obs", None, "src", None),
    )
    return jax.shard_map(
        functools.partial(per_device, mesh.shape["obs"], mesh.shape["src"]),
        mesh=mesh,
        in_specs=placed,
        out_specs=P(None, ("obs", "src"), None, None),
        check_vma=False,
    )
```

```python
import functools

import jax
import jax.numpy as jnp
from jax import lax
from jax.experimental import pallas as pl
from jax.experimental.pallas import tpu as pltpu
from jax.sharding import PartitionSpec as P

MESH = pl.DeviceIdType.MESH
F32 = jnp.float32
BF16 = jnp.bfloat16
NT = (((1,), (1,)), ((), ()))


def flipped(me, bits, count):
    other = me
    place = 1
    while place < count:
        if bits & place:
            other = other + (1 - 2 * ((me // place) % 2)) * place
        place *= 2
    return other


def partner(me, turn, count):
    if count & (count - 1) == 0:
        return flipped(me, count - turn, count)
    return lax.rem(me + turn, count)


def kernel(n_obs, n_src, hist_ref, inc_ref, proj_ref, expand_ref, near_ref, coup_ref, lag_ref, out_ref,
           hv, av, pv, nv, cv, cf, wv, yv, xn, bv, mv, qh, qn, sendp, recvp, base, ov,
           load_sem, out_sem, hs_sem, hr_sem, qs_sem, qr_sem, ps_sem, pr_sem):
    o = lax.axis_index("obs")
    s = lax.axis_index("src")
    hist, clusters, excite, unknowns = hist_ref.shape
    steps = inc_ref.shape[0]
    rank = proj_ref.shape[1]
    width = clusters * rank
    sources = lag_ref.shape[2]
    tile = 256

    barrier = pltpu.get_barrier_semaphore()
    src_peers = [partner(s, turn, n_src) for turn in range(1, n_src)]
    obs_peers = [partner(o, turn, n_obs) for turn in range(1, n_obs)]
    for peer in src_peers:
        pl.semaphore_signal(barrier, inc=1, device_id=(o, peer), device_id_type=MESH)
    for peer in obs_peers:
        pl.semaphore_signal(barrier, inc=1, device_id=(peer, s), device_id_type=MESH)

    loads = []

    def load(src, dst):
        copy = pltpu.make_async_copy(src, dst, load_sem.at[len(loads)])
        copy.start()
        loads.append(copy)
        return copy

    def rows(index, size):
        return pl.ds(index * size, size)

    h_loads = [load(proj_ref.at[c], pv.at[c, rows(c, rank)]) for c in range(clusters)]
    h_loads += [load(hist_ref.at[k, c], hv.at[c, rows(k, excite)]) for c in range(clusters) for k in range(hist)]
    c_loads = [load(coup_ref, cv)]
    n_loads = []
    for c in range(clusters):
        mine = [load(inc_ref.at[t, c], av.at[c, rows(t, excite)]) for t in range(steps)]
        mine.append(load(expand_ref.at[c], av.at[c, rows(steps, excite)]))
        mine.append(load(near_ref.at[c], nv.at[c]))
        n_loads.append(mine)

    for c in range(clusters):
        for k in range(clusters):
            if k != c:
                pv[c, k * rank:(k + 1) * rank] = jnp.zeros((rank, unknowns), BF16)
                xn[c, k * rank:(k + 1) * rank] = jnp.zeros((rank, unknowns), BF16)

    for copy in h_loads:
        copy.wait()
    past = jnp.zeros((hist * excite, width), F32)
    for c in range(clusters):
        past = past + lax.dot_general(hv[c], pv[c], NT, preferred_element_type=F32)
    qh[s] = past.astype(BF16)
    pl.semaphore_wait(barrier, n_src + n_obs - 2)

    def h_copy(turn, slot):
        return pltpu.make_async_remote_copy(
            src_ref=qh.at[slot], dst_ref=qh.at[slot], send_sem=hs_sem.at[turn], recv_sem=hr_sem.at[slot],
            device_id=(o, src_peers[turn]), device_id_type=MESH)

    def q_copy(step, turn, slot):
        return pltpu.make_async_remote_copy(
            src_ref=qn.at[step, slot], dst_ref=qn.at[step, slot], send_sem=qs_sem.at[step, turn],
            recv_sem=qr_sem.at[step, slot], device_id=(o, src_peers[turn]), device_id_type=MESH)

    def p_copy(step, turn, at, slot):
        return pltpu.make_async_remote_copy(
            src_ref=sendp.at[step, at], dst_ref=recvp.at[step, slot], send_sem=ps_sem.at[step, turn],
            recv_sem=pr_sem.at[step, slot], device_id=(obs_peers[turn], s), device_id_type=MESH)

    group = 2 if n_src % 2 == 0 else 1
    for turn in range(n_src - 1):
        h_copy(turn, s).start()

    for copy in c_loads:
        copy.wait()
    lane = lax.broadcasted_iota(jnp.int32, (rank, width), 1)

    def build(j, carry):
        for p in range(2):
            cf[p] = cv[p, pl.ds(pl.multiple_of(j * (rank * n_obs), rank * n_obs), rank * n_obs), :].astype(F32)
        at = pl.ds(pl.multiple_of(j * rank, rank), rank)
        for to in range(n_obs):
            lag = jnp.full((rank, width), lag_ref[to, 0, j], jnp.int32)
            for k in range(1, clusters):
                lag = jnp.where(lane >= k * rank, lag_ref[to, k, j], lag)
            first = cf[0, pl.ds(to, rank, stride=n_obs), :]
            second = cf[1, pl.ds(to, rank, stride=n_obs), :]
            zero = jnp.zeros_like(first)
            one, two = lag == 1, lag == 2
            cols = slice(to * width, (to + 1) * width)
            wv[0, at, cols] = jnp.where(one, first, zero).astype(BF16)
            wv[1, at, cols] = jnp.where(two, first, jnp.where(one, second, zero)).astype(BF16)
            wv[2, at, cols] = jnp.where(two, second, zero).astype(BF16)
        return carry

    lax.fori_loop(0, sources, build, 0)

    def near(c):
        for copy in n_loads[c]:
            copy.wait()

        def column(j, carry):
            at = pl.ds(pl.multiple_of(j * tile, tile), tile)
            value = jnp.dot(av[c], nv[c, :, at], preferred_element_type=F32)
            yv[c, :, at] = value
            xn[c, c * rank:(c + 1) * rank, at] = value[steps * excite:].astype(BF16)
            return carry

        lax.fori_loop(0, unknowns // tile, column, 0)
        return lax.dot_general(yv[c].astype(BF16), pv[c], NT, preferred_element_type=F32)

    def keep(c, value):
        if c == 0:
            bv[...] = value[:steps * excite]
        else:
            bv[...] += value[:steps * excite]
        mv[c * rank:(c + 1) * rank] = value[steps * excite:].astype(BF16)

    keep(0, near(0))

    for turn in range(n_src - 1):
        h_copy(turn, src_peers[turn]).wait_recv()

    pairs = n_src // group
    own_pair = s // group
    ordered = [own_pair] + [partner(own_pair, turn, pairs) for turn in range(pairs - 1, 0, -1)]

    def gathered(ref):
        return jnp.concatenate([ref[k] for k in range(n_src)], axis=1)

    def newest_term(step, total):
        for place, pair in enumerate(ordered):
            for k in range(group):
                if place > 0:
                    q_copy(step, 0, pair * group + k).wait_recv()
                elif group == 2 and k == 0:
                    q_copy(step, 0, partner_slot).wait_recv()
            part = jnp.concatenate([qn[step, pair * group + k] for k in range(group)], axis=1)
            deep = group * width
            rows_at = pl.ds(pl.multiple_of(pair * deep, deep), deep)
            total = total + jnp.dot(part, wv[0, rows_at, :], preferred_element_type=F32)
        return total

    partner_slot = own_pair * 2 + (1 - s % 2)

    def slot_of(ref, k):
        return jnp.concatenate([ref[j, k * excite:(k + 1) * excite] for j in range(n_src)], axis=1)

    older = [slot_of(qh, k) for k in range(hist)]

    def send_partial(step, total):
        for to in range(n_obs):
            sendp[step, to] = total[:, to * width:(to + 1) * width].astype(BF16)
        for turn in range(n_obs - 1):
            p_copy(step, turn, obs_peers[turn], o).start()

    total = jnp.dot(older[hist - 1], wv[0], preferred_element_type=F32)
    for d in range(2, hist + 1):
        total = total + jnp.dot(older[hist - d], wv[d - 1], preferred_element_type=F32)
    send_partial(0, total)

    for ahead in range(1, hist):
        total = None
        for d in range(ahead + 1, hist + 1):
            term = jnp.dot(older[hist + ahead - d], wv[d - 1], preferred_element_type=F32)
            total = term if total is None else total + term
        base[ahead] = total
    for ahead in range(hist, steps):
        base[ahead] = jnp.zeros((excite, n_obs * width), F32)

    for c in range(1, clusters):
        keep(c, near(c))

    outs = []

    def finish(step, field):
        for c in range(clusters):
            far = jnp.dot(field, xn[c], preferred_element_type=F32)
            ov[step, c] = (yv[c, step * excite:(step + 1) * excite] - far).astype(BF16)
            copy = pltpu.make_async_copy(ov.at[step, c], out_ref.at[step, c], out_sem.at[step, c])
            copy.start()
            outs.append(copy)

    for step in range(steps):
        field = sendp[step, o].astype(F32)
        for turn in range(n_obs - 1):
            p_copy(step, turn, 0, obs_peers[turn]).wait_recv()
            field = field + recvp[step, obs_peers[turn]].astype(F32)
        field = field.astype(BF16)
        if step + 1 == steps:
            finish(step, field)
            break
        newest = bv[step * excite:(step + 1) * excite] - jnp.dot(field, mv[...], preferred_element_type=F32)
        qn[step, s] = newest.astype(BF16)
        for turn in range(n_src - 1):
            q_copy(step, turn, s).start()
        finish(step, field)
        send_partial(step + 1, newest_term(step, base[step + 1]))
        columns = gathered(qn.at[step])
        for d in range(2, hist + 1):
            if step + d < steps:
                base[step + d] += jnp.dot(columns, wv[d - 1], preferred_element_type=F32)

    for copy in outs:
        copy.wait()
    for turn in range(n_src - 1):
        h_copy(turn, s).wait_send()
    for step in range(steps):
        for turn in range(n_obs - 1):
            p_copy(step, turn, obs_peers[turn], o).wait_send()
        if step + 1 < steps:
            for turn in range(n_src - 1):
                q_copy(step, turn, s).wait_send()


def hand_on(made_ref, out_ref, held, in_sem, out_sem):
    steps, clusters = made_ref.shape[:2]
    places = [(t, c) for t in range(steps) for c in range(clusters)]
    taken = [pltpu.make_async_copy(made_ref.at[t, c], held.at[t, c], in_sem.at[t, c]) for t, c in places]
    given = [pltpu.make_async_copy(held.at[t, c], out_ref.at[t, c], out_sem.at[t, c]) for t, c in places]
    for copy in taken:
        copy.start()
    for before, after in zip(taken, given):
        before.wait()
        after.start()
    for copy in given:
        copy.wait()


def per_device(n_obs, n_src, history, incident, proj_basis, expand_basis, near_inverse, couplings, lags):
    hist, clusters, excite, unknowns = history.shape
    steps = incident.shape[0]
    rank = proj_basis.shape[1]
    width = clusters * rank
    taps, src_rows = couplings.shape[:2]
    sources = lags.shape[0]
    obs_cols = n_obs * width
    flat = couplings.reshape(taps, src_rows * n_obs, width)
    lag_table = jnp.transpose(lags.reshape(sources, n_obs, clusters), (1, 2, 0))
    stacked = (steps + 1) * excite
    loads = clusters * (1 + hist + steps + 2) + 1
    any_spec = pl.BlockSpec(memory_space=pl.ANY)
    dma = pltpu.SemaphoreType.DMA
    made = pl.pallas_call(
        functools.partial(kernel, n_obs, n_src),
        out_shape=jax.ShapeDtypeStruct(incident.shape, BF16),
        in_specs=[any_spec] * 6 + [pl.BlockSpec(memory_space=pltpu.SMEM)],
        out_specs=any_spec,
        scratch_shapes=[
            pltpu.VMEM((clusters, hist * excite, unknowns), BF16),
            pltpu.VMEM((clusters, stacked, unknowns), BF16),
            pltpu.VMEM((clusters, width, unknowns), BF16),
            pltpu.VMEM((clusters, unknowns, unknowns), BF16),
            pltpu.VMEM((taps, src_rows * n_obs, width), BF16),
            pltpu.VMEM((taps, rank * n_obs, width), F32),
            pltpu.VMEM((hist, src_rows, obs_cols), BF16),
            pltpu.VMEM((clusters, stacked, unknowns), F32),
            pltpu.VMEM((clusters, width, unknowns), BF16),
            pltpu.VMEM((steps * excite, width), F32),
            pltpu.VMEM((width, width), BF16),
            pltpu.VMEM((n_src, hist * excite, width), BF16),
            pltpu.VMEM((steps - 1, n_src, excite, width), BF16),
            pltpu.VMEM((steps, n_obs, excite, width), BF16),
            pltpu.VMEM((steps, n_obs, excite, width), BF16),
            pltpu.VMEM((steps, excite, obs_cols), F32),
            pltpu.VMEM((steps, clusters, excite, unknowns), BF16),
            dma((loads,)),
            dma((steps, clusters)),
            dma((n_src,)),
            dma((n_src,)),
            dma((steps - 1, n_src)),
            dma((steps - 1, n_src)),
            dma((steps, n_obs)),
            dma((steps, n_obs)),
        ],
        compiler_params=pltpu.CompilerParams(
            collective_id=0, has_side_effects=True, vmem_limit_bytes=63000 * 1024
        ),
    )(history, incident, proj_basis, expand_basis, near_inverse, flat, lag_table)
    return pl.pallas_call(
        hand_on,
        out_shape=jax.ShapeDtypeStruct(incident.shape, BF16),
        in_specs=[any_spec],
        out_specs=any_spec,
        scratch_shapes=[pltpu.VMEM(incident.shape, BF16), dma((steps, clusters)), dma((steps, clusters))],
        compiler_params=pltpu.CompilerParams(vmem_limit_bytes=63000 * 1024),
    )(made)


def solution(mesh):
    placed = (
        P(None, ("obs", "src"), None, None),
        P(None, ("obs", "src"), None, None),
        P(("obs", "src"), None, None),
        P(("obs", "src"), None, None),
        P(("obs", "src"), None, None),
        P(None, "obs", None, "src", None),
        P("obs", None, "src", None),
    )
    return jax.shard_map(
        functools.partial(per_device, mesh.shape["obs"], mesh.shape["src"]),
        mesh=mesh,
        in_specs=placed,
        out_specs=P(None, ("obs", "src"), None, None),
        check_vma=False,
    )
```
